256 devices in a mesh: ctx: 8 (over x, core), ch: 32 (over y, z).
Axes of the slice: x: 4, y: 4, z: 8, core: 2. Of those that a mesh axis runs over, the one named last changes fastest.
Arguments:
- out_grad: bfloat16 [2048, 8192], P('ctx', 'ch'), may hold values from -6 to 6
- out_weight: bfloat16 [8192, 8192], P(None, 'ch'), may hold values from -0.125 to 0.125
- query_in: bfloat16 [2048, 8192], P('ctx', 'ch'), may hold values from -6 to 6
- conv_out: bfloat16 [2048, 8192], P('ctx', 'ch'), may hold values from -6 to 6
- residues: float32 [8192, 16], P('ch'), may hold values from -0.3 to 0.3
- decay_rates: float32 [8192, 16], P('ch'), may hold values from 0.96 to 1, as said below
Outputs:
- grad_query: bfloat16 [2048, 8192], P('ctx', 'ch')
- grad_input: bfloat16 [2048, 8192], P('ctx', 'ch')
The draws below stay inside these ranges and needn't reach their ends.
Inputs may be any that keep to these rules, and one draw needn't show every extreme that they name: `decay_rates`: each pole lies strictly below 1.
All inputs are finite; a program needn't handle non-finite values.
Results may differ from the reference program's by a relative error of at most 0.001.
Values may be sent and summed in bfloat16 or wider, within the bound.
A program may use at most 128 MiB of HBM per device.

```python
import math
import jax
import jax.numpy as jnp
from jax import lax

D = 8192
N_MODES = 16
TOKENS = 2048


def draw_decay_rates(key, part):
    lowest = math.log(0.2 / TOKENS)
    highest = math.log(1.0 / 30.0)
    mixing = jax.random.uniform(key, (D, N_MODES), jnp.float32)
    return jnp.exp(-jnp.exp(lowest + mixing * (highest - lowest)))


def raised(values, rng, source, target, shards_of, factor):
    owner, partner = [(jnp.arange(values.shape[dim]) // (values.shape[dim] // shards_of)).reshape([-1 if axis == dim else 1 for axis in range(values.ndim)]) for dim in (source, target)]
    chosen = jax.random.permutation(rng, shards_of)[partner]
    strong = (owner == chosen) | (owner == (partner + shards_of // 2) % shards_of)
    return jnp.where(strong, factor * values, values)


def steps_of(key, dims, shards, smallest, high):
    factor_of = 1.0
    for axis_at, shards_of in shards:
        steps = jax.random.uniform(jax.random.fold_in(jax.random.fold_in(key, 6), axis_at), (shards_of,), jnp.float32, smallest / len(shards), high / len(shards))
        factor_of = factor_of * jnp.repeat(jnp.exp(steps), dims[axis_at] // shards_of).reshape((-1,) + (1,) * (len(dims) - 1 - axis_at))
    return factor_of


def gaussian(own_key, shape, scale, limit, shards=(), kind=jnp.bfloat16):
    result = jax.random.normal(own_key, shape, jnp.float32) * scale
    if len(shards) > 0:
        result = steps_of(own_key, shape, shards, -0.22, 0.18) * result
    return jnp.clip(result, min=-limit, max=limit).astype(kind)


def noise_with(stream_key, extent, deviation, limit, shards, heavy, dtype=jnp.bfloat16):
    array = deviation * jax.random.normal(stream_key, extent, jnp.float32)
    if shards:
        array = array * steps_of(stream_key, extent, shards, -0.22, 0.18)
    return jnp.clip(raised(array, jax.random.fold_in(stream_key, 3), *heavy), -limit, limit).astype(dtype)


def setup_inputs(seed: int = 0) -> dict:
    seeds = jax.random.split(jax.random.key(seed), 7)
    out_grad = gaussian(seeds[0], (TOKENS, D), 1.0, 6.0, ((0, 8), (1, 32)))
    out_weight = noise_with(seeds[1], (D, D), D ** -0.5, 0.125, ((1, 32),), (1, 0, 32, 2.75))
    query_in = gaussian(seeds[2], (TOKENS, D), 1.0, 6.0, ((0, 8), (1, 32)))
    conv_out = gaussian(seeds[3], (TOKENS, D), 1.0, 6.0, ((0, 8), (1, 32)))
    residues = gaussian(seeds[4], (D, N_MODES), 0.05, 0.3, ((0, 32),), jnp.float32)
    decay_rates = draw_decay_rates(jax.random.fold_in(seeds[6], 71), 0)
    return {"out_grad": out_grad, "out_weight": out_weight, "query_in": query_in, "conv_out": conv_out, "residues": residues, "decay_rates": decay_rates}


def reference(out_grad, out_weight, query_in, conv_out, residues, decay_rates):
    grad_mix = jnp.dot(out_grad, out_weight.T, preferred_element_type=jnp.float32)
    grad_query = (grad_mix * conv_out.astype(jnp.float32)).astype(jnp.bfloat16)
    grad_conv = grad_mix * query_in.astype(jnp.float32)

    def backstep(adjoint, conv_row):
        adjoint = decay_rates * adjoint + conv_row[:, None]
        return adjoint, jnp.sum(residues * adjoint, axis=1)

    start_state = jnp.zeros(decay_rates.shape, jnp.float32)
    final_state, grad_rows = lax.scan(backstep, start_state, grad_conv, reverse=True)
    return grad_query, grad_rows.astype(jnp.bfloat16)
```

```python
import jax
import jax.numpy as jnp
from jax import lax
from jax.experimental import pallas as pl
from jax.experimental.pallas import tpu as pltpu
from jax.sharding import PartitionSpec as P

MESH = pl.DeviceIdType.MESH
NY, NZ, NX, NCTX = 4, 8, 4, 8
SEG = 8
LANES = 128


def kernel(
    g_hbm, w_hbm, q_hbm, v_hbm, r_ref, a_ref,
    gq_hbm, gi_hbm,
    gbuf, wbuf, pbuf, hbuf, rbuf, qbuf, vbuf, gc, yf, gqb, gib,
    ab, rb, m1, m2, m4, a7, bpow, sown, sall,
    lsem, asend, arecv, gsend, grecv, xsend, xrecv, ysend, yrecv, ssend, srecv,
):
    f32 = jnp.float32
    ctx = lax.axis_index("ctx")
    ch = lax.axis_index("ch")
    y = ch // NZ
    z = ch % NZ
    tok = gq_hbm.shape[0]
    wid = gq_hbm.shape[1]
    modes = a_ref.shape[0]
    steps = tok // SEG

    def at_z(d):
        return (ctx, y * NZ + (z + d + NZ) % NZ)

    def at_y(d):
        return (ctx, ((y + d + NY) % NY) * NZ + z)

    def at_ctx(d):
        return ((ctx + d + NCTX) % NCTX, ch)

    twin = ctx + 1 - 2 * (ctx % 2)
    at_twin = (twin, ch)

    locals_ = [
        pltpu.make_async_copy(g_hbm, gbuf.at[0], lsem.at[0]),
        pltpu.make_async_copy(q_hbm, qbuf, lsem.at[1]),
        pltpu.make_async_copy(v_hbm, vbuf, lsem.at[2]),
    ]
    for dy in range(NY):
        first = (((y + dy) % NY) * NZ + z) * NCTX
        locals_.append(
            pltpu.make_async_copy(w_hbm.at[pl.ds(first, NCTX)], wbuf.at[dy, :, 0], lsem.at[3 + dy])
        )
    for c in locals_:
        c.start()

    barrier = pltpu.get_barrier_semaphore()
    peers = [at_z(d) for d in range(1, NZ)] + [at_y(1), at_y(-1)]
    peers += [at_ctx(d) for d in range(1, NCTX)]
    for p in peers:
        pl.semaphore_signal(barrier, inc=1, device_id=p, device_id_type=MESH)
    pl.semaphore_wait(barrier, len(peers))

    def rcopy(src, dst, ssem, rsem, dev):
        return pltpu.make_async_remote_copy(
            src_ref=src, dst_ref=dst, send_sem=ssem, recv_sem=rsem, device_id=dev, device_id_type=MESH
        )

    def spread(dy):
        for o in range(1, NZ):
            zz = (z - o + NZ) % NZ
            row = (((y + dy) % NY) * NZ + zz) * NCTX + ctx
            rcopy(w_hbm.at[row], wbuf.at[dy, ctx, o], asend.at[dy], arecv.at[dy], at_z(-o)).start()

    def block(dy, who, lo, n):
        return wbuf.at[dy, who, pl.ds(lo, n)]

    full = (1, NZ - 1)
    part_a = (1, 4)
    part_b = (5, 3)
    back = (ctx + NCTX - 2) % NCTX
    ahead = (ctx + 2) % NCTX
    far = (ctx + 4) % NCTX
    links = {
        0: (ctx, full, at_ctx(2)),
        1: (ctx, full, at_ctx(-2)),
        2: (back, part_a, at_ctx(2)),
        3: (ahead, part_b, at_ctx(-2)),
        4: (ctx, full, at_twin),
        5: (back, full, at_twin),
        6: (ahead, full, at_twin),
        7: (far, part_a, at_twin),
        8: (far, part_b, at_twin),
    }
    tback = (twin + NCTX - 2) % NCTX
    tahead = (twin + 2) % NCTX
    tfar = (twin + 4) % NCTX
    lands = {
        0: (back, full), 1: (ahead, full), 2: (far, part_a), 3: (far, part_b),
        4: (twin, full), 5: (tback, full), 6: (tahead, full), 7: (tfar, part_a), 8: (tfar, part_b),
    }

    def xcopy(dy, k):
        who, part, dev = links[k]
        ref = block(dy, who, *part)
        return rcopy(ref, ref, xsend.at[dy, k], xrecv.at[dy, k], dev)

    def xwait(dy, k):
        who, part = lands[k]
        ref = block(dy, who, *part)
        rcopy(ref, ref, xsend.at[dy, k], xrecv.at[dy, k], at_twin).wait_recv()

    def share0(dy):
        ref = block(dy, ctx, *full)
        rcopy(ref, ref, asend.at[dy], arecv.at[dy], at_twin).wait_recv()
        for k in (0, 1, 4):
            xcopy(dy, k).start()

    def share1(dy):
        xwait(dy, 0)
        xcopy(dy, 2).start()
        xcopy(dy, 5).start()
        xwait(dy, 1)
        xcopy(dy, 3).start()
        xcopy(dy, 6).start()

    def share2(dy):
        xwait(dy, 2)
        xcopy(dy, 7).start()
        xwait(dy, 3)
        xcopy(dy, 8).start()

    def share3(dy):
        for k in (4, 5, 6, 7, 8):
            xwait(dy, k)

    half = tok // 2
    lo_rows = pl.ds(0, half)
    hi_rows = pl.ds(half, half)

    def gcopy(k):
        if k < 3:
            src, dst, dev = (0, NZ - 1, 1) if k == 0 else (NZ - k, NZ - k - 1, 1)
        elif k == 3:
            return rcopy(gbuf.at[5, lo_rows], gbuf.at[4, lo_rows], gsend.at[3], grecv.at[3], at_z(1))
        elif k < 7:
            src, dst, dev = k - 4, k - 3, -1
        else:
            return rcopy(gbuf.at[3, hi_rows], gbuf.at[4, hi_rows], gsend.at[7], grecv.at[7], at_z(-1))
        source = g_hbm if src == 0 else gbuf.at[src]
        return rcopy(source, gbuf.at[dst], gsend.at[k], grecv.at[k], at_z(dev))

    def gather0():
        gcopy(0).start()
        gcopy(4).start()

    def gather(h):
        gcopy(h - 1).wait_recv()
        gcopy(h).start()
        gcopy(h + 3).wait_recv()
        gcopy(h + 4).start()

    def gather_done():
        gcopy(3).wait_recv()
        gcopy(7).wait_recv()

    spread(2)
    spread(1)
    gather0()

    a_t = a_ref[...]
    r_t = r_ref[...]
    seg = lax.broadcasted_iota(jnp.int32, (SEG, wid), 0)
    for n in range(modes):
        a1 = jnp.broadcast_to(a_t[n : n + 1], (SEG, wid))
        ab[n] = a1
        rb[n] = jnp.broadcast_to(r_t[n : n + 1], (SEG, wid))
        p = a1
        for _ in range(5):
            p = p * p
        p2 = p * p
        p4 = p2 * p2
        m1[n] = jnp.where(seg < SEG - 1, p, 0.0)
        m2[n] = jnp.where(seg < SEG - 2, p2, 0.0)
        m4[n] = jnp.where(seg < SEG - 4, p4, 0.0)
        left = SEG - 1 - seg
        a7[n] = (
            jnp.where(left % 2 == 1, p, 1.0)
            * jnp.where((left // 2) % 2 == 1, p2, 1.0)
            * jnp.where(left // 4 == 1, p4, 1.0)
        )
    b = a_t
    for _ in range(8):
        b = b * b
    bpow[...] = b

    def partial(dy):
        g = jnp.concatenate([gbuf[o] for o in range(NZ)], axis=1)
        w = jnp.concatenate([wbuf[dy, :, o].reshape(wid, wid) for o in range(NZ)], axis=1)
        return lax.dot_general(g, w, (((1,), (1,)), ((), ())), preferred_element_type=f32)

    share0(2)
    gather(1)
    share0(1)
    share1(2)
    gather(2)
    spread(3)
    share1(1)
    share2(2)
    gather(3)
    spread(0)
    share2(1)
    share3(2)
    for c in locals_:
        c.wait()
    gather_done()

    pbuf[2] = partial(2)
    far0 = rcopy(pbuf.at[2, lo_rows], hbuf.at[0], ysend.at[0], yrecv.at[0], at_y(1))
    far1 = rcopy(pbuf.at[2, hi_rows], hbuf.at[1], ysend.at[1], yrecv.at[1], at_y(-1))
    far0.start()
    far1.start()
    share0(3)
    share3(1)
    pbuf[1] = partial(1)
    share1(3)
    share0(0)
    far0.wait_recv()
    pbuf[1, lo_rows] += hbuf[0]
    near0 = rcopy(pbuf.at[1], rbuf.at[0], ysend.at[2], yrecv.at[2], at_y(1))
    near0.start()
    share2(3)
    share1(0)
    share3(3)
    pbuf[3] = partial(3)
    far1.wait_recv()
    pbuf[3, hi_rows] += hbuf[1]
    near1 = rcopy(pbuf.at[3], rbuf.at[1], ysend.at[3], yrecv.at[3], at_y(-1))
    near1.start()
    share2(0)
    share3(0)
    pbuf[0] = partial(0)
    near0.wait_recv()
    near1.wait_recv()

    mix = pbuf[0] + rbuf[0] + rbuf[1]
    conv = mix * qbuf[...].astype(f32)
    for col in range(0, wid, LANES):
        gc[col // LANES] = conv[:, col : col + LANES]
    gqb[...] = (mix * vbuf[...].astype(f32)).astype(jnp.bfloat16)
    out_q = pltpu.make_async_copy(gqb, gq_hbm, lsem.at[7])
    out_q.start()

    lanes = LANES
    unroll = 8

    def sweep(j, state, poles, col):
        row = gc[col // lanes, pl.ds(j, SEG, stride=steps)]
        return [poles[n] * state[n] + row for n in range(modes)]

    ends = []
    for col in range(0, wid, lanes):
        cols = slice(col, col + lanes)
        poles = [ab[n, :, cols] for n in range(modes)]

        def first(k, state, poles=poles, col=col):
            state = list(state)
            for u in range(unroll):
                state = sweep(steps - 1 - (k * unroll + u), state, poles, col)
            return tuple(state)

        zero = tuple(jnp.zeros((SEG, lanes), f32) for _ in range(modes))
        state = lax.fori_loop(0, steps // unroll, first, zero)
        for n in range(modes):
            s = state[n]
            s = s + m1[n, :, cols] * pltpu.roll(s, SEG - 1, 0)
            s = s + m2[n, :, cols] * pltpu.roll(s, SEG - 2, 0)
            s = s + m4[n, :, cols] * pltpu.roll(s, SEG - 4, 0)
            sown[pl.ds(n, 1), cols] = s[0:1]
            ends.append(jnp.where(seg[:, :lanes] < SEG - 1, pltpu.roll(s, SEG - 1, 0), 0.0))
    for t in range(len(ends)):
        col = (t // modes) * lanes
        m1[t % modes, :, col : col + lanes] = ends[t]

    states = [
        rcopy(sown, sall.at[NCTX - d], ssend.at[d], srecv.at[NCTX - d], at_ctx(d))
        for d in range(1, NCTX)
    ]
    for s in states:
        s.start()
    incoming = jnp.zeros((modes, wid), f32)
    for d in range(NCTX - 1, 0, -1):
        rcopy(sown, sall.at[d], ssend.at[d], srecv.at[d], at_ctx(d)).wait_recv()
        here = jnp.where(ctx + d < NCTX, 1.0, 0.0).astype(f32)
        incoming = bpow[...] * incoming + here * sall[d]

    for col in range(0, wid, lanes):
        cols = slice(col, col + lanes)
        poles = [ab[n, :, cols] for n in range(modes)]
        gains = [rb[n, :, cols] for n in range(modes)]
        state = tuple(
            m1[n, :, cols] + a7[n, :, cols] * incoming[n : n + 1, cols] for n in range(modes)
        )

        def second(k, state, poles=poles, gains=gains, col=col):
            state = list(state)
            for u in range(unroll):
                j = steps - 1 - (k * unroll + u)
                state = sweep(j, state, poles, col)
                terms = [gains[n] * state[n] for n in range(modes)]
                while len(terms) > 1:
                    terms = [terms[m] + terms[m + 1] for m in range(0, len(terms), 2)]
                yf[col // lanes, pl.ds(j, SEG, stride=steps)] = terms[0]
            return tuple(state)

        lax.fori_loop(0, steps // unroll, second, state)
    for col in range(0, wid, lanes):
        gib[:, col : col + lanes] = yf[col // lanes].astype(jnp.bfloat16)
    out_i = pltpu.make_async_copy(gib, gi_hbm, lsem.at[8])
    out_i.start()

    for dy in range(NY):
        ref = block(dy, ctx, *full)
        rcopy(ref, ref, asend.at[dy], arecv.at[dy], at_twin).wait_send()
        for k in range(9):
            xcopy(dy, k).wait_send()
    for k in range(8):
        gcopy(k).wait_send()
    for c in (far0, far1, near0, near1):
        c.wait_send()
    for s in states:
        s.wait_send()
    out_q.wait()
    out_i.wait()


def local(out_grad, out_weight, query_in, conv_out, residues, decay_rates):
    tok, wid = query_in.shape
    modes = residues.shape[1]
    bf16, f32 = jnp.bfloat16, jnp.float32
    chunk = wid // NCTX
    w = out_weight.reshape(out_weight.shape[0] // chunk, chunk, out_weight.shape[1])
    any_ = pl.BlockSpec(memory_space=pl.ANY)
    vm = pl.BlockSpec(memory_space=pltpu.VMEM)
    dma = pltpu.SemaphoreType.DMA
    table = pltpu.VMEM((modes, SEG, wid), f32)
    return pl.pallas_call(
        kernel,
        out_shape=(
            jax.ShapeDtypeStruct((tok, wid), bf16),
            jax.ShapeDtypeStruct((tok, wid), bf16),
        ),
        in_specs=[any_, any_, any_, any_, vm, vm],
        out_specs=(any_, any_),
        scratch_shapes=[
            pltpu.VMEM((NZ, tok, wid), bf16),
            pltpu.VMEM((NY, NCTX, NZ, chunk, wid), bf16),
            pltpu.VMEM((NY, tok, wid), f32),
            pltpu.VMEM((2, tok // 2, wid), f32),
            pltpu.VMEM((2, tok, wid), f32),
            pltpu.VMEM((tok, wid), bf16),
            pltpu.VMEM((tok, wid), bf16),
            pltpu.VMEM((wid // LANES, tok, LANES), f32),
            pltpu.VMEM((wid // LANES, tok, LANES), f32),
            pltpu.VMEM((tok, wid), bf16),
            pltpu.VMEM((tok, wid), bf16),
            table, table, table, table, table, table,
            pltpu.VMEM((modes, wid), f32),
            pltpu.VMEM((modes, wid), f32),
            pltpu.VMEM((NCTX, modes, wid), f32),
            dma((9,)),
            dma((NY,)), dma((NY,)),
            dma((8,)), dma((8,)),
            dma((NY, 9)), dma((NY, 9)),
            dma((4,)), dma((4,)),
            dma((NCTX,)), dma((NCTX,)),
        ],
        compiler_params=pltpu.CompilerParams(
            collective_id=0, has_side_effects=True
        ),
        name="mix_and_scan",
    )(out_grad, w, query_in, conv_out, residues.T, decay_rates.T)


def solution(mesh):
    placed = (
        P("ctx", "ch"),
        P(None, "ch"),
        P("ctx", "ch"),
        P("ctx", "ch"),
        P("ch", None),
        P("ch", None),
    )
    return jax.shard_map(
        local,
        mesh=mesh,
        in_specs=placed,
        out_specs=(P("ctx", "ch"), P("ctx", "ch")),
        check_vma=False,
    )
```

```python
import jax
import jax.numpy as jnp
from jax import lax
from jax.experimental import pallas as pl
from jax.experimental.pallas import tpu as pltpu
from jax.sharding import PartitionSpec as P

MESH = pl.DeviceIdType.MESH
NY, NZ, NX, NCTX = 4, 8, 4, 8
SEG = 8
LANES = 128
UNROLL = 8
NH = 2
FIRST = ((0, 2), (0, 1), (0, 3), (1, 0), (1, 1))
ARRIVED, SHARED, GATHERED, SUMMED, ADDED, SPREAD = range(6)
EVENTS = (
    (0, 2, 0), (1, 2, 2), (0, 1, 0), (1, 2, 0), (1, 2, 1), (1, 2, 3), (2, 0, 0), (5, 0, 0), (2, 0, 4),
    (1, 2, 5), (0, 3, 0), (1, 1, 0), (1, 1, 2), (2, 1, 0), (2, 1, 4), (1, 1, 1), (1, 1, 3), (1, 2, 4),
    (2, 0, 1), (1, 3, 2), (1, 3, 0), (1, 3, 3), (1, 3, 1), (2, 0, 5), (1, 1, 5), (1, 1, 4), (1, 3, 5),
    (2, 1, 1), (2, 1, 5), (0, 0, 0), (1, 3, 4), (2, 0, 2), (2, 0, 6), (1, 0, 2), (2, 1, 2), (2, 1, 6),
    (1, 0, 0), (1, 0, 1), (1, 0, 3), (2, 0, 3), (3, 2, 0), (3, 1, 0), (3, 3, 0), (1, 0, 5), (2, 1, 7),
    (3, 2, 1), (3, 1, 1), (3, 3, 1), (1, 0, 4), (3, 0, 0), (3, 0, 1), (4, 0, 0), (4, 0, 1), (4, 1, 0),
    (4, 1, 1),
)


def sweep(gc, j, state, poles, col):
    row = gc[col // LANES, pl.ds(j, SEG, stride=gc.shape[1] // SEG)]
    return [p * s + row for p, s in zip(poles, state)]


def kernel(
    g_hbm, w_hbm, q_hbm, v_hbm, r_hbm, a_hbm,
    gqb, gc, ab, rb, start,
    gbuf, wbuf, pbuf, hbuf, rbuf, qbuf, vbuf, r_ref, a_ref,
    m1, m2, m4, a7, bpow, sown, sall,
    lsem, asend, arecv, gsend, grecv, xsend, xrecv, ysend, yrecv, ssend, srecv,
):
    f32 = jnp.float32
    ctx = lax.axis_index("ctx")
    ch = lax.axis_index("ch")
    y = ch // NZ
    z = ch % NZ
    tok, wid = q_hbm.shape
    modes = a_hbm.shape[0]
    steps = tok // SEG

    def at_z(d):
        return (ctx, y * NZ + (z + d + NZ) % NZ)

    def at_y(d):
        return (ctx, ((y + d + NY) % NY) * NZ + z)

    def at_ctx(d):
        return ((ctx + d + NCTX) % NCTX, ch)

    twin = ctx + 1 - 2 * (ctx % 2)
    at_twin = (twin, ch)

    locals_ = [
        pltpu.make_async_copy(g_hbm, gbuf.at[0], lsem.at[0]),
        pltpu.make_async_copy(q_hbm, qbuf, lsem.at[1]),
        pltpu.make_async_copy(v_hbm, vbuf, lsem.at[2]),
    ]
    for dy in range(NY):
        first = (((y + dy) % NY) * NZ + z) * NCTX
        locals_.append(
            pltpu.make_async_copy(w_hbm.at[pl.ds(first, NCTX)], wbuf.at[dy, :, 0], lsem.at[3 + dy])
        )
    poles_in = [
        pltpu.make_async_copy(r_hbm, r_ref, lsem.at[7]),
        pltpu.make_async_copy(a_hbm, a_ref, lsem.at[8]),
    ]
    for c in locals_ + poles_in:
        c.start()

    barrier = pltpu.get_barrier_semaphore()
    peers = [at_z(d) for d in range(1, NZ)] + [at_y(1), at_y(-1)]
    peers += [at_ctx(d) for d in range(1, NCTX)]
    for p in peers:
        pl.semaphore_signal(barrier, inc=1, device_id=p, device_id_type=MESH)
    pl.semaphore_wait(barrier, len(peers))

    def rcopy(src, dst, ssem, rsem, dev):
        return pltpu.make_async_remote_copy(
            src_ref=src, dst_ref=dst, send_sem=ssem, recv_sem=rsem, device_id=dev, device_id_type=MESH
        )

    def spread(dy):
        for o in range(1, NZ):
            zz = (z - o + NZ) % NZ
            row = (((y + dy) % NY) * NZ + zz) * NCTX + ctx
            rcopy(w_hbm.at[row], wbuf.at[dy, ctx, o], asend.at[dy], arecv.at[dy], at_z(-o)).start()

    def block(dy, who, lo, n):
        return wbuf.at[dy, who, pl.ds(lo, n)]

    full = (1, NZ - 1)
    part_a = (1, 4)
    part_b = (5, 3)

    def beside(who):
        return (who + NCTX - 2) % NCTX, (who + 2) % NCTX, (who + 4) % NCTX

    back, ahead, far_off = beside(ctx)
    up, down = at_ctx(2), at_ctx(-2)
    links = (
        (ctx, part_a, up), (ctx, part_b, up), (ctx, part_b, down), (ctx, part_a, down),
        (back, part_a, up), (ahead, part_b, down),
        (ctx, full, at_twin), (back, part_a, at_twin), (back, part_b, at_twin), (ahead, part_b, at_twin),
        (ahead, part_a, at_twin), (far_off, part_a, at_twin), (far_off, part_b, at_twin),
    )
    tback, tahead, tfar = beside(twin)
    lands = (
        (back, part_a), (back, part_b), (ahead, part_b), (ahead, part_a),
        (far_off, part_a), (far_off, part_b),
        (twin, full), (tback, part_a), (tback, part_b), (tahead, part_b),
        (tahead, part_a), (tfar, part_a), (tfar, part_b),
    )

    def xcopy(dy, k):
        who, part, dev = links[k]
        ref = block(dy, who, *part)
        return rcopy(ref, ref, xsend.at[dy, k], xrecv.at[dy, k], dev)

    def xwait(dy, k):
        who, part = lands[k]
        ref = block(dy, who, *part)
        rcopy(ref, ref, xsend.at[dy, k], xrecv.at[dy, k], at_twin).wait_recv()

    def arrived(dy):
        ref = block(dy, ctx, *full)
        rcopy(ref, ref, asend.at[dy], arecv.at[dy], at_twin).wait_recv()
        for k in (0, 2, 1, 3, 6):
            xcopy(dy, k).start()

    def shared(dy, k):
        xwait(dy, k)
        if k == 0:
            xcopy(dy, 4).start()
        if k == 2:
            xcopy(dy, 5).start()
        xcopy(dy, 7 + k).start()

    half = tok // NH
    quarter = half // 2

    def rows(h):
        return pl.ds(h * half, half)

    def gcopy(h, k):
        up = k < 4
        hop = k % 4
        src = (NZ - hop) % NZ if up else hop
        dst = NZ - hop - 1 if up else hop + 1
        source = g_hbm if hop == 0 else gbuf.at[src]
        return rcopy(
            source.at[rows(h)], gbuf.at[dst, rows(h)], gsend.at[h, k], grecv.at[h, k], at_z(1 if up else -1)
        )

    def last(h):
        return 3 if h < NH // 2 else 7

    def gather0(h):
        gcopy(h, 0).start()
        gcopy(h, 4).start()

    def gathered(h, k):
        gcopy(h, k).wait_recv()
        if k % 4 < 2 or k + 1 == last(h):
            gcopy(h, k + 1).start()

    for kind, n in FIRST:
        gather0(n) if kind else spread(n)

    for c in poles_in:
        c.wait()
    a_t = a_ref[...]
    r_t = r_ref[...]
    seg = lax.broadcasted_iota(jnp.int32, (SEG, wid), 0)
    for n in range(modes):
        a1 = jnp.broadcast_to(a_t[n : n + 1], (SEG, wid))
        ab[n] = a1
        rb[n] = jnp.broadcast_to(r_t[n : n + 1], (SEG, wid))
        p = a1
        for _ in range(5):
            p = p * p
        p2 = p * p
        p4 = p2 * p2
        m1[n] = jnp.where(seg < SEG - 1, p, 0.0)
        m2[n] = jnp.where(seg < SEG - 2, p2, 0.0)
        m4[n] = jnp.where(seg < SEG - 4, p4, 0.0)
        left = SEG - 1 - seg
        a7[n] = (
            jnp.where(left % 2 == 1, p, 1.0)
            * jnp.where((left // 2) % 2 == 1, p2, 1.0)
            * jnp.where(left // 4 == 1, p4, 1.0)
        )
    b = a_t
    for _ in range(8):
        b = b * b
    bpow[...] = b

    def partial(dy, h):
        g = jnp.concatenate([gbuf[o, rows(h)] for o in range(NZ)], axis=1)
        w = jnp.concatenate([wbuf[dy, :, o].reshape(wid, wid) for o in range(NZ)], axis=1)
        pbuf[dy, rows(h)] = lax.dot_general(
            g, w, (((1,), (1,)), ((), ())), preferred_element_type=f32
        )

    def quart(h, side):
        return pl.ds(h * half + side * quarter, quarter)

    def far(h, side):
        return rcopy(
            pbuf.at[2, quart(h, side)], hbuf.at[side, h],
            ysend.at[0, side, h], yrecv.at[0, side, h], at_y(1 - 2 * side),
        )

    def near(h, side, late):
        part = quart(h, side if late else 1 - side)
        return rcopy(
            pbuf.at[1 + 2 * side, part], rbuf.at[side, part],
            ysend.at[1 + late, side, h], yrecv.at[1 + late, side, h], at_y(1 - 2 * side),
        )

    def summed(dy, h):
        partial(dy, h)
        if dy == 2:
            far(h, 0).start()
            far(h, 1).start()
        elif dy:
            near(h, dy // 2, 0).start()

    def added(h, side):
        far(h, side).wait_recv()
        pbuf[1 + 2 * side, quart(h, side)] += hbuf[side, h]
        near(h, side, 1).start()

    here = False
    whole = set()
    for what, a, b in EVENTS:
        if what == ARRIVED:
            arrived(a)
        elif what == SHARED:
            shared(a, b)
        elif what == GATHERED:
            gathered(a, b)
        elif what == ADDED:
            added(a, b)
        elif what == SPREAD:
            spread(a)
        else:
            if not here:
                for c in locals_:
                    c.wait()
                here = True
            if a not in whole:
                whole.add(a)
                for k in range(6, 13):
                    xwait(a, k)
            summed(a, b)
    for h in range(NH):
        for side in range(2):
            near(h, side, 0).wait_recv()
            near(h, side, 1).wait_recv()

    mix = pbuf[0] + rbuf[0] + rbuf[1]
    conv = mix * qbuf[...].astype(f32)
    for col in range(0, wid, LANES):
        gc[col // LANES] = conv[:, col : col + LANES]
    gqb[...] = (mix * vbuf[...].astype(f32)).astype(jnp.bfloat16)
    lanes = LANES

    ends = []
    for col in range(0, wid, lanes):
        cols = slice(col, col + lanes)
        poles = [ab[n, :, cols] for n in range(modes)]

        def first(k, state, poles=poles, col=col):
            state = list(state)
            for u in range(UNROLL):
                state = sweep(gc, steps - 1 - (k * UNROLL + u), state, poles, col)
            return tuple(state)

        zero = tuple(jnp.zeros((SEG, lanes), f32) for _ in range(modes))
        state = lax.fori_loop(0, steps // UNROLL, first, zero)
        for n in range(modes):
            s = state[n]
            s = s + m1[n, :, cols] * pltpu.roll(s, SEG - 1, 0)
            s = s + m2[n, :, cols] * pltpu.roll(s, SEG - 2, 0)
            s = s + m4[n, :, cols] * pltpu.roll(s, SEG - 4, 0)
            sown[pl.ds(n, 1), cols] = s[0:1]
            ends.append(jnp.where(seg[:, :lanes] < SEG - 1, pltpu.roll(s, SEG - 1, 0), 0.0))
    states = [
        rcopy(sown, sall.at[NCTX - d], ssend.at[d], srecv.at[NCTX - d], at_ctx(d))
        for d in range(1, NCTX)
    ]
    for s in states:
        s.start()
    incoming = jnp.zeros((modes, wid), f32)
    for d in range(NCTX - 1, 0, -1):
        rcopy(sown, sall.at[d], ssend.at[d], srecv.at[d], at_ctx(d)).wait_recv()
        here = jnp.where(ctx + d < NCTX, 1.0, 0.0).astype(f32)
        incoming = bpow[...] * incoming + here * sall[d]

    for t in range(len(ends)):
        n, col = t % modes, (t // modes) * lanes
        cols = slice(col, col + lanes)
        start[n, :, cols] = ends[t] + a7[n, :, cols] * incoming[n : n + 1, cols]

    for dy in range(NY):
        ref = block(dy, ctx, *full)
        rcopy(ref, ref, asend.at[dy], arecv.at[dy], at_twin).wait_send()
        for k in range(13):
            xcopy(dy, k).wait_send()
    for k in range(8):
        for h in range(NH):
            if k % 4 < 3 or k == last(h):
                gcopy(h, k).wait_send()
    for h in range(NH):
        for side in range(2):
            far(h, side).wait_send()
            near(h, side, 0).wait_send()
            near(h, side, 1).wait_send()
    for s in states:
        s.wait_send()


def finish(gqb, gc, ab, rb, start, gq_hbm, gi_hbm, yf, gib, sem):
    modes, _, wid = ab.shape
    steps = gqb.shape[0] // SEG
    out_q = pltpu.make_async_copy(gqb, gq_hbm, sem.at[0])
    out_q.start()
    for col in range(0, wid, LANES):
        cols = slice(col, col + LANES)
        poles = [ab[n, :, cols] for n in range(modes)]
        gains = [rb[n, :, cols] for n in range(modes)]

        def second(k, state, poles=poles, gains=gains, col=col):
            state = list(state)
            for u in range(UNROLL):
                j = steps - 1 - (k * UNROLL + u)
                state = sweep(gc, j, state, poles, col)
                terms = [gains[n] * state[n] for n in range(modes)]
                while len(terms) > 1:
                    terms = [terms[m] + terms[m + 1] for m in range(0, len(terms), 2)]
                yf[col // LANES, pl.ds(j, SEG, stride=steps)] = terms[0]
            return tuple(state)

        lax.fori_loop(0, steps // UNROLL, second, tuple(start[n, :, cols] for n in range(modes)))
        gib[:, cols] = yf[col // LANES].astype(gib.dtype)
    out_i = pltpu.make_async_copy(gib, gi_hbm, sem.at[1])
    out_i.start()
    out_q.wait()
    out_i.wait()


def local(out_grad, out_weight, query_in, conv_out, residues, decay_rates):
    tok, wid = query_in.shape
    modes = residues.shape[1]
    bf16, f32 = jnp.bfloat16, jnp.float32
    chunk = wid // NCTX
    w = out_weight.reshape(out_weight.shape[0] // chunk, chunk, out_weight.shape[1])
    any_ = pl.BlockSpec(memory_space=pltpu.HBM)
    vm = pl.BlockSpec(memory_space=pltpu.VMEM)
    dma = pltpu.SemaphoreType.DMA
    table = pltpu.VMEM((modes, SEG, wid), f32)
    full = jax.ShapeDtypeStruct((tok, wid), bf16)
    tall = jax.ShapeDtypeStruct((modes, SEG, wid), f32)
    inputs = (out_grad, w, query_in, conv_out, residues.T, decay_rates.T)
    held = pl.pallas_call(
        kernel,
        out_shape=(full, jax.ShapeDtypeStruct((wid // LANES, tok, LANES), f32), tall, tall, tall),
        in_specs=[any_] * 6,
        out_specs=(vm,) * 5,
        scratch_shapes=[
            pltpu.VMEM((NZ, tok, wid), bf16),
            pltpu.VMEM((NY, NCTX, NZ, chunk, wid), bf16),
            pltpu.VMEM((NY, tok, wid), f32),
            pltpu.VMEM((2, NH, tok // NH // 2, wid), f32),
            pltpu.VMEM((2, tok, wid), f32),
            pltpu.VMEM((tok, wid), bf16),
            pltpu.VMEM((tok, wid), bf16),
            pltpu.VMEM((modes, wid), f32),
            pltpu.VMEM((modes, wid), f32),
            table, table, table, table,
            pltpu.VMEM((modes, wid), f32),
            pltpu.VMEM((modes, wid), f32),
            pltpu.VMEM((NCTX, modes, wid), f32),
            dma((9,)),
            dma((NY,)), dma((NY,)),
            dma((NH, 8)), dma((NH, 8)),
            dma((NY, 13)), dma((NY, 13)),
            dma((3, 2, NH)), dma((3, 2, NH)),
            dma((NCTX,)), dma((NCTX,)),
        ],
        compiler_params=pltpu.CompilerParams(
            collective_id=0, has_side_effects=True, vmem_limit_bytes=55_000_000
        ),
        name="mix",
    )(*[pltpu.with_memory_space_constraint(t, pltpu.HBM) for t in inputs])
    return pl.pallas_call(
        finish,
        out_shape=(full, full),
        in_specs=[vm] * 5,
        out_specs=(any_, any_),
        scratch_shapes=[
            pltpu.VMEM((wid // LANES, tok, LANES), f32),
            pltpu.VMEM((tok, wid), bf16),
            dma((2,)),
        ],
        compiler_params=pltpu.CompilerParams(vmem_limit_bytes=16 * 1024 * 1024),
        name="finish",
    )(*held)


def solution(mesh):
    placed = (
        P("ctx", "ch"),
        P(None, "ch"),
        P("ctx", "ch"),
        P("ctx", "ch"),
        P("ch", None),
        P("ch", None),
    )
    return jax.shard_map(
        local,
        mesh=mesh,
        in_specs=placed,
        out_specs=(P("ctx", "ch"), P("ctx", "ch")),
        check_vma=False,
    )
```

```python
import jax
import jax.numpy as jnp
from jax import lax
from jax.experimental import pallas as pl
from jax.experimental.pallas import tpu as pltpu
from jax.sharding import PartitionSpec as P

MESH = pl.DeviceIdType.MESH
NY, NZ, NX, NCTX = 4, 8, 4, 8
SEG = 8
LANES = 128
UNROLL = 8
NH = 2
CHUNKS = ((0, 4, True), (4, 4, False))
FIRST = ((0, 2), (0, 1), (0, 3), (1, 0), (1, 1))
ARRIVED, SHARED, GATHERED, SUMMED, ADDED, SPREAD = range(6)
EVENTS = (
    (0, 2, 0), (1, 2, 2), (0, 1, 0), (1, 2, 0), (1, 2, 1), (1, 2, 3), (2, 0, 0), (5, 0, 0), (2, 0, 4),
    (1, 2, 5), (0, 3, 0), (1, 1, 0), (2, 1, 0), (2, 1, 4), (1, 1, 2), (1, 1, 1), (2, 0, 1), (1, 1, 3),
    (1, 2, 4), (1, 3, 2), (1, 3, 0), (1, 3, 3), (2, 0, 5), (1, 3, 1), (1, 1, 5), (2, 1, 1), (2, 1, 5),
    (1, 1, 4), (1, 3, 5), (0, 0, 0), (2, 0, 2), (2, 0, 6), (1, 3, 4), (2, 1, 2), (2, 1, 6), (1, 0, 2),
    (1, 0, 0), (2, 0, 3), (3, 2, 0), (3, 1, 0), (3, 3, 0), (1, 0, 3), (1, 0, 1), (2, 1, 7), (3, 2, 1),
    (3, 1, 1), (3, 3, 1), (1, 0, 5), (1, 0, 4), (4, 0, 0), (4, 0, 1), (3, 0, 0), (3, 0, 1), (4, 1, 0),
    (4, 1, 1),
)


def sweep(gc, j, state, poles, col):
    row = gc[col // LANES, pl.ds(j, SEG, stride=gc.shape[1] // SEG)]
    return [p * s + row for p, s in zip(poles, state)]


def kernel(
    g_hbm, w_hbm, q_hbm, v_hbm, r_hbm, a_hbm,
    gqb, gc, ab, rb, start,
    gbuf, wbuf, pbuf, hbuf, rbuf, qbuf, vbuf, r_ref, a_ref,
    m1, m2, m4, a7, bpow, sown, sall,
    lsem, asend, arecv, gsend, grecv, xsend, xrecv, ysend, yrecv, ssend, srecv,
):
    f32 = jnp.float32
    ctx = lax.axis_index("ctx")
    ch = lax.axis_index("ch")
    y = ch // NZ
    z = ch % NZ
    tok, wid = q_hbm.shape
    modes = a_hbm.shape[0]
    steps = tok // SEG

    def at_z(d):
        return (ctx, y * NZ + (z + d + NZ) % NZ)

    def at_y(d):
        return (ctx, ((y + d + NY) % NY) * NZ + z)

    def at_ctx(d):
        return ((ctx + d + NCTX) % NCTX, ch)

    twin = ctx + 1 - 2 * (ctx % 2)
    at_twin = (twin, ch)

    locals_ = [
        pltpu.make_async_copy(g_hbm, gbuf.at[0], lsem.at[0]),
        pltpu.make_async_copy(q_hbm, qbuf, lsem.at[1]),
        pltpu.make_async_copy(v_hbm, vbuf, lsem.at[2]),
    ]
    for dy in range(NY):
        first = (((y + dy) % NY) * NZ + z) * NCTX
        locals_.append(
            pltpu.make_async_copy(w_hbm.at[pl.ds(first, NCTX)], wbuf.at[dy, :, 0], lsem.at[3 + dy])
        )
    poles_in = [
        pltpu.make_async_copy(r_hbm, r_ref, lsem.at[7]),
        pltpu.make_async_copy(a_hbm, a_ref, lsem.at[8]),
    ]
    barrier = pltpu.get_barrier_semaphore()
    peers = [at_z(d) for d in range(1, NZ)] + [at_y(1), at_y(-1)]
    peers += [at_ctx(d) for d in range(1, NCTX)]
    for p in peers:
        pl.semaphore_signal(barrier, inc=1, device_id=p, device_id_type=MESH)
    for c in locals_ + poles_in:
        c.start()
    pl.semaphore_wait(barrier, len(peers))

    def rcopy(src, dst, ssem, rsem, dev):
        return pltpu.make_async_remote_copy(
            src_ref=src, dst_ref=dst, send_sem=ssem, recv_sem=rsem, device_id=dev, device_id_type=MESH
        )

    def spread(dy):
        for o in (4, 3, 5, 2, 6, 1, 7):
            zz = (z - o + NZ) % NZ
            row = (((y + dy) % NY) * NZ + zz) * NCTX + ctx
            rcopy(w_hbm.at[row], wbuf.at[dy, ctx, o], asend.at[dy], arecv.at[dy], at_z(-o)).start()

    def block(dy, who, lo, n):
        return wbuf.at[dy, who, pl.ds(lo, n)]

    full = (1, NZ - 1)
    part_a = (1, 4)
    part_b = (5, 3)

    def beside(who):
        return (who + NCTX - 2) % NCTX, (who + 2) % NCTX, (who + 4) % NCTX

    back, ahead, far_off = beside(ctx)
    up, down = at_ctx(2), at_ctx(-2)
    links = (
        (ctx, part_a, up), (ctx, part_b, up), (ctx, part_b, down), (ctx, part_a, down),
        (back, part_a, up), (ahead, part_b, down),
        (ctx, full, at_twin), (back, part_a, at_twin), (back, part_b, at_twin), (ahead, part_b, at_twin),
        (ahead, part_a, at_twin), (far_off, part_a, at_twin), (far_off, part_b, at_twin),
    )
    tback, tahead, tfar = beside(twin)
    lands = (
        (back, part_a), (back, part_b), (ahead, part_b), (ahead, part_a),
        (far_off, part_a), (far_off, part_b),
        (twin, full), (tback, part_a), (tback, part_b), (tahead, part_b),
        (tahead, part_a), (tfar, part_a), (tfar, part_b),
    )

    def xcopy(dy, k):
        who, part, dev = links[k]
        ref = block(dy, who, *part)
        return rcopy(ref, ref, xsend.at[dy, k], xrecv.at[dy, k], dev)

    def xwait(dy, k):
        who, part = lands[k]
        ref = block(dy, who, *part)
        rcopy(ref, ref, xsend.at[dy, k], xrecv.at[dy, k], at_twin).wait_recv()

    def arrived(dy):
        ref = block(dy, ctx, *full)
        rcopy(ref, ref, asend.at[dy], arecv.at[dy], at_twin).wait_recv()
        for k in (0, 2, 1, 3, 6):
            xcopy(dy, k).start()

    def shared(dy, k):
        xwait(dy, k)
        if k == 0:
            xcopy(dy, 4).start()
        if k == 2:
            xcopy(dy, 5).start()
        xcopy(dy, 7 + k).start()

    eighth = tok // 8

    def rows(h):
        first, n, _ = CHUNKS[h]
        return pl.ds(first * eighth, n * eighth)

    def gcopy(h, k):
        up = k < 4
        hop = k % 4
        src = (NZ - hop) % NZ if up else hop
        dst = NZ - hop - 1 if up else hop + 1
        source = g_hbm if hop == 0 else gbuf.at[src]
        return rcopy(
            source.at[rows(h)], gbuf.at[dst, rows(h)], gsend.at[h, k], grecv.at[h, k], at_z(1 if up else -1)
        )

    def last(h):
        return 3 if CHUNKS[h][2] else 7

    def gather0(h):
        gcopy(h, 0).start()
        gcopy(h, 4).start()

    def gathered(h, k):
        gcopy(h, k).wait_recv()
        if k % 4 < 2 or k + 1 == last(h):
            gcopy(h, k + 1).start()

    for kind, n in FIRST:
        gather0(n) if kind else spread(n)

    for c in poles_in:
        c.wait()
    a_t = a_ref[...]
    r_t = r_ref[...]
    seg = lax.broadcasted_iota(jnp.int32, (SEG, wid), 0)
    for n in range(modes):
        a1 = jnp.broadcast_to(a_t[n : n + 1], (SEG, wid))
        ab[n] = a1
        rb[n] = jnp.broadcast_to(r_t[n : n + 1], (SEG, wid))
        p = a1
        for _ in range(5):
            p = p * p
        p2 = p * p
        p4 = p2 * p2
        m1[n] = jnp.where(seg < SEG - 1, p, 0.0)
        m2[n] = jnp.where(seg < SEG - 2, p2, 0.0)
        m4[n] = jnp.where(seg < SEG - 4, p4, 0.0)
        left = SEG - 1 - seg
        a7[n] = (
            jnp.where(left % 2 == 1, p, 1.0)
            * jnp.where((left // 2) % 2 == 1, p2, 1.0)
            * jnp.where(left // 4 == 1, p4, 1.0)
        )
    b = a_t
    for _ in range(8):
        b = b * b
    bpow[...] = b

    def partial(dy, h):
        g = jnp.concatenate([gbuf[o, rows(h)] for o in range(NZ)], axis=1)
        w = jnp.concatenate([wbuf[dy, :, o].reshape(wid, wid) for o in range(NZ)], axis=1)
        pbuf[dy, rows(h)] = lax.dot_general(
            g, w, (((1,), (1,)), ((), ())), preferred_element_type=f32
        )

    def quart(h, side):
        first, n, _ = CHUNKS[h]
        return pl.ds(first * eighth + side * (n * eighth // 2), n * eighth // 2)

    def far(h, side):
        return rcopy(
            pbuf.at[2, quart(h, side)], hbuf.at[side, quart(h, 0)],
            ysend.at[0, side, h], yrecv.at[0, side, h], at_y(1 - 2 * side),
        )

    def near(h, side, late):
        part = quart(h, side if late else 1 - side)
        return rcopy(
            pbuf.at[1 + 2 * side, part], rbuf.at[side, part],
            ysend.at[1 + late, side, h], yrecv.at[1 + late, side, h], at_y(1 - 2 * side),
        )

    def summed(dy, h):
        partial(dy, h)
        if dy == 2:
            far(h, 0).start()
            far(h, 1).start()
        elif dy:
            near(h, dy // 2, 0).start()

    def added(h, side):
        far(h, side).wait_recv()
        pbuf[1 + 2 * side, quart(h, side)] += hbuf[side, quart(h, 0)]
        near(h, side, 1).start()

    here = False
    whole = set()
    for what, a, b in EVENTS:
        if what == ARRIVED:
            arrived(a)
        elif what == SHARED:
            shared(a, b)
        elif what == GATHERED:
            gathered(a, b)
        elif what == ADDED:
            added(a, b)
        elif what == SPREAD:
            spread(a)
        else:
            if not here:
                for c in locals_:
                    c.wait()
                here = True
            if a not in whole:
                whole.add(a)
                for k in range(6, 13):
                    xwait(a, k)
            summed(a, b)
    for h in range(NH):
        for side in range(2):
            near(h, side, 0).wait_recv()
            near(h, side, 1).wait_recv()

    mix = pbuf[0] + rbuf[0] + rbuf[1]
    conv = mix * qbuf[...].astype(f32)
    for col in range(0, wid, LANES):
        gc[col // LANES] = conv[:, col : col + LANES]
    gqb[...] = (mix * vbuf[...].astype(f32)).astype(jnp.bfloat16)
    lanes = LANES

    ends = []
    for col in range(0, wid, lanes):
        cols = slice(col, col + lanes)
        poles = [ab[n, :, cols] for n in range(modes)]

        def first(k, state, poles=poles, col=col):
            state = list(state)
            for u in range(UNROLL):
                state = sweep(gc, steps - 1 - (k * UNROLL + u), state, poles, col)
            return tuple(state)

        zero = tuple(jnp.zeros((SEG, lanes), f32) for _ in range(modes))
        state = lax.fori_loop(0, steps // UNROLL, first, zero)
        for n in range(modes):
            s = state[n]
            s = s + m1[n, :, cols] * pltpu.roll(s, SEG - 1, 0)
            s = s + m2[n, :, cols] * pltpu.roll(s, SEG - 2, 0)
            s = s + m4[n, :, cols] * pltpu.roll(s, SEG - 4, 0)
            sown[pl.ds(n, 1), cols] = s[0:1]
            ends.append(jnp.where(seg[:, :lanes] < SEG - 1, pltpu.roll(s, SEG - 1, 0), 0.0))
    states = [
        rcopy(sown, sall.at[NCTX - d], ssend.at[d], srecv.at[NCTX - d], at_ctx(d))
        for d in range(1, NCTX)
    ]
    for s in states:
        s.start()
    incoming = jnp.zeros((modes, wid), f32)
    for d in range(NCTX - 1, 0, -1):
        rcopy(sown, sall.at[d], ssend.at[d], srecv.at[d], at_ctx(d)).wait_recv()
        here = jnp.where(ctx + d < NCTX, 1.0, 0.0).astype(f32)
        incoming = bpow[...] * incoming + here * sall[d]

    for t in range(len(ends)):
        n, col = t % modes, (t // modes) * lanes
        cols = slice(col, col + lanes)
        start[n, :, cols] = ends[t] + a7[n, :, cols] * incoming[n : n + 1, cols]

    for dy in range(NY):
        ref = block(dy, ctx, *full)
        rcopy(ref, ref, asend.at[dy], arecv.at[dy], at_twin).wait_send()
        for k in range(13):
            xcopy(dy, k).wait_send()
    for k in range(8):
        for h in range(NH):
            if k % 4 < 3 or k == last(h):
                gcopy(h, k).wait_send()
    for h in range(NH):
        for side in range(2):
            far(h, side).wait_send()
            near(h, side, 0).wait_send()
            near(h, side, 1).wait_send()
    for s in states:
        s.wait_send()


def finish(gqb, gc, ab, rb, start, gq_hbm, gi_hbm, yf, gib, sem):
    modes, _, wid = ab.shape
    steps = gqb.shape[0] // SEG
    out_q = pltpu.make_async_copy(gqb, gq_hbm, sem.at[0])
    out_q.start()
    for col in range(0, wid, LANES):
        cols = slice(col, col + LANES)
        poles = [ab[n, :, cols] for n in range(modes)]
        gains = [rb[n, :, cols] for n in range(modes)]

        def second(k, state, poles=poles, gains=gains, col=col):
            state = list(state)
            for u in range(UNROLL):
                j = steps - 1 - (k * UNROLL + u)
                state = sweep(gc, j, state, poles, col)
                terms = [gains[n] * state[n] for n in range(modes)]
                while len(terms) > 1:
                    terms = [terms[m] + terms[m + 1] for m in range(0, len(terms), 2)]
                yf[col // LANES, pl.ds(j, SEG, stride=steps)] = terms[0]
            return tuple(state)

        lax.fori_loop(0, steps // UNROLL, second, tuple(start[n, :, cols] for n in range(modes)))
        gib[:, cols] = yf[col // LANES].astype(gib.dtype)
    out_i = pltpu.make_async_copy(gib, gi_hbm, sem.at[1])
    out_i.start()
    out_q.wait()
    out_i.wait()


def local(out_grad, out_weight, query_in, conv_out, residues, decay_rates):
    tok, wid = query_in.shape
    modes = residues.shape[1]
    bf16, f32 = jnp.bfloat16, jnp.float32
    chunk = wid // NCTX
    w = out_weight.reshape(out_weight.shape[0] // chunk, chunk, out_weight.shape[1])
    any_ = pl.BlockSpec(memory_space=pltpu.HBM)
    vm = pl.BlockSpec(memory_space=pltpu.VMEM)
    dma = pltpu.SemaphoreType.DMA
    table = pltpu.VMEM((modes, SEG, wid), f32)
    full = jax.ShapeDtypeStruct((tok, wid), bf16)
    tall = jax.ShapeDtypeStruct((modes, SEG, wid), f32)
    inputs = (out_grad, w, query_in, conv_out, residues.T, decay_rates.T)
    held = pl.pallas_call(
        kernel,
        out_shape=(full, jax.ShapeDtypeStruct((wid // LANES, tok, LANES), f32), tall, tall, tall),
        in_specs=[any_] * 6,
        out_specs=(vm,) * 5,
        scratch_shapes=[
            pltpu.VMEM((NZ, tok, wid), bf16),
            pltpu.VMEM((NY, NCTX, NZ, chunk, wid), bf16),
            pltpu.VMEM((NY, tok, wid), f32),
            pltpu.VMEM((2, tok, wid), f32),
            pltpu.VMEM((2, tok, wid), f32),
            pltpu.VMEM((tok, wid), bf16),
            pltpu.VMEM((tok, wid), bf16),
            pltpu.VMEM((modes, wid), f32),
            pltpu.VMEM((modes, wid), f32),
            table, table, table, table,
            pltpu.VMEM((modes, wid), f32),
            pltpu.VMEM((modes, wid), f32),
            pltpu.VMEM((NCTX, modes, wid), f32),
            dma((9,)),
            dma((NY,)), dma((NY,)),
            dma((NH, 8)), dma((NH, 8)),
            dma((NY, 13)), dma((NY, 13)),
            dma((3, 2, NH)), dma((3, 2, NH)),
            dma((NCTX,)), dma((NCTX,)),
        ],
        compiler_params=pltpu.CompilerParams(
            collective_id=0, has_side_effects=True, vmem_limit_bytes=55_000_000
        ),
        name="mix",
    )(*[pltpu.with_memory_space_constraint(t, pltpu.HBM) for t in inputs])
    return pl.pallas_call(
        finish,
        out_shape=(full, full),
        in_specs=[vm] * 5,
        out_specs=(any_, any_),
        scratch_shapes=[
            pltpu.VMEM((wid // LANES, tok, LANES), f32),
            pltpu.VMEM((tok, wid), bf16),
            dma((2,)),
        ],
        compiler_params=pltpu.CompilerParams(vmem_limit_bytes=16 * 1024 * 1024),
        name="finish",
    )(*held)


def solution(mesh):
    placed = (
        P("ctx", "ch"),
        P(None, "ch"),
        P("ctx", "ch"),
        P("ctx", "ch"),
        P("ch", None),
        P("ch", None),
    )
    return jax.shard_map(
        local,
        mesh=mesh,
        in_specs=placed,
        out_specs=(P("ctx", "ch"), P("ctx", "ch")),
        check_vma=False,
    )
```

```python
import jax
import jax.numpy as jnp
from jax import lax
from jax.experimental import pallas as pl
from jax.experimental.pallas import tpu as pltpu
from jax.sharding import PartitionSpec as P

MESH = pl.DeviceIdType.MESH
NY, NZ, NX, NCTX = 4, 8, 4, 8
SEG = 8
LANES = 128
UNROLL = 8
NH = 2
CHUNKS = ((0, 4, True), (4, 4, False))
FIRST = ((0, 2), (0, 1), (0, 3), (1, 0), (1, 1))
ARRIVED, SHARED, GATHERED, SUMMED, ADDED, SPREAD = range(6)
EVENTS = (
    (0, 2, 0), (1, 2, 2), (0, 1, 0), (1, 2, 0), (2, 0, 0), (5, 0, 0), (2, 0, 4), (1, 2, 1), (1, 2, 3),
    (2, 1, 0), (2, 1, 4), (1, 2, 5), (0, 3, 0), (1, 1, 0), (2, 0, 1), (1, 1, 2), (1, 1, 1), (1, 1, 3),
    (1, 2, 4), (1, 3, 2), (2, 0, 5), (1, 3, 0), (1, 3, 3), (2, 1, 1), (2, 1, 5), (1, 3, 1), (1, 1, 5),
    (2, 0, 2), (2, 0, 6), (1, 1, 4), (1, 3, 5), (0, 0, 0), (2, 1, 2), (2, 1, 6), (1, 3, 4), (2, 0, 3),
    (3, 2, 0), (3, 1, 0), (3, 3, 0), (1, 0, 2), (1, 0, 0), (2, 1, 7), (3, 2, 1), (3, 1, 1), (3, 3, 1),
    (4, 0, 0), (4, 0, 1), (4, 1, 0), (4, 1, 1), (1, 0, 5), (1, 0, 4), (1, 0, 3), (1, 0, 1), (3, 0, 0),
    (3, 0, 1),
)


def sweep(gc, j, state, poles, col):
    row = gc[col // LANES, pl.ds(j, SEG, stride=gc.shape[1] // SEG)]
    return [p * s + row for p, s in zip(poles, state)]


def total(terms):
    while len(terms) > 1:
        terms = [terms[m] + terms[m + 1] for m in range(0, len(terms), 2)]
    return terms[0]


def kernel(
    g_hbm, w_hbm, q_hbm, v_hbm, r_hbm, a_hbm,
    gqb, yf, ab, start,
    gc, rb, gbuf, wbuf, pbuf, hbuf, rbuf, qbuf, vbuf, r_ref, a_ref,
    m1, m2, m4, a7, bpow, sown, sall,
    lsem, asend, arecv, gsend, grecv, xsend, xrecv, ysend, yrecv, ssend, srecv,
):
    f32 = jnp.float32
    ctx = lax.axis_index("ctx")
    ch = lax.axis_index("ch")
    y = ch // NZ
    z = ch % NZ
    tok, wid = q_hbm.shape
    modes = a_hbm.shape[0]
    steps = tok // SEG

    def at_z(d):
        return (ctx, y * NZ + (z + d + NZ) % NZ)

    def at_y(d):
        return (ctx, ((y + d + NY) % NY) * NZ + z)

    def at_ctx(d):
        return ((ctx + d + NCTX) % NCTX, ch)

    twin = ctx + 1 - 2 * (ctx % 2)
    at_twin = (twin, ch)

    locals_ = [
        pltpu.make_async_copy(g_hbm, gbuf.at[0], lsem.at[0]),
        pltpu.make_async_copy(q_hbm, qbuf, lsem.at[1]),
        pltpu.make_async_copy(v_hbm, vbuf, lsem.at[2]),
    ]
    for dy in range(NY):
        first = (((y + dy) % NY) * NZ + z) * NCTX
        locals_.append(
            pltpu.make_async_copy(w_hbm.at[pl.ds(first, NCTX)], wbuf.at[dy, :, 0], lsem.at[3 + dy])
        )
    poles_in = [
        pltpu.make_async_copy(r_hbm, r_ref, lsem.at[7]),
        pltpu.make_async_copy(a_hbm, a_ref, lsem.at[8]),
    ]
    barrier = pltpu.get_barrier_semaphore()
    peers = [at_z(d) for d in range(1, NZ)] + [at_y(1), at_y(-1)]
    peers += [at_ctx(d) for d in range(1, NCTX)]
    for p in peers:
        pl.semaphore_signal(barrier, inc=1, device_id=p, device_id_type=MESH)
    for c in locals_ + poles_in:
        c.start()
    pl.semaphore_wait(barrier, len(peers))

    def rcopy(src, dst, ssem, rsem, dev):
        return pltpu.make_async_remote_copy(
            src_ref=src, dst_ref=dst, send_sem=ssem, recv_sem=rsem, device_id=dev, device_id_type=MESH
        )

    def spread(dy):
        for o in (4, 3, 5, 2, 6, 1, 7):
            zz = (z - o + NZ) % NZ
            row = (((y + dy) % NY) * NZ + zz) * NCTX + ctx
            rcopy(w_hbm.at[row], wbuf.at[dy, ctx, o], asend.at[dy], arecv.at[dy], at_z(-o)).start()

    def block(dy, who, lo, n):
        return wbuf.at[dy, who, pl.ds(lo, n)]

    full = (1, NZ - 1)
    part_a = (1, 4)
    part_b = (5, 3)

    def beside(who):
        return (who + NCTX - 2) % NCTX, (who + 2) % NCTX, (who + 4) % NCTX

    back, ahead, far_off = beside(ctx)
    up, down = at_ctx(2), at_ctx(-2)
    links = (
        (ctx, part_a, up), (ctx, part_b, up), (ctx, part_b, down), (ctx, part_a, down),
        (back, part_a, up), (ahead, part_b, down),
        (ctx, full, at_twin), (back, part_a, at_twin), (back, part_b, at_twin), (ahead, part_b, at_twin),
        (ahead, part_a, at_twin), (far_off, part_a, at_twin), (far_off, part_b, at_twin),
    )
    tback, tahead, tfar = beside(twin)
    lands = (
        (back, part_a), (back, part_b), (ahead, part_b), (ahead, part_a),
        (far_off, part_a), (far_off, part_b),
        (twin, full), (tback, part_a), (tback, part_b), (tahead, part_b),
        (tahead, part_a), (tfar, part_a), (tfar, part_b),
    )

    def xcopy(dy, k):
        who, part, dev = links[k]
        ref = block(dy, who, *part)
        return rcopy(ref, ref, xsend.at[dy, k], xrecv.at[dy, k], dev)

    def xwait(dy, k):
        who, part = lands[k]
        ref = block(dy, who, *part)
        rcopy(ref, ref, xsend.at[dy, k], xrecv.at[dy, k], at_twin).wait_recv()

    def arrived(dy):
        ref = block(dy, ctx, *full)
        rcopy(ref, ref, asend.at[dy], arecv.at[dy], at_twin).wait_recv()
        for k in (0, 2, 1, 3, 6):
            xcopy(dy, k).start()

    def shared(dy, k):
        xwait(dy, k)
        if k == 0:
            xcopy(dy, 4).start()
        if k == 2:
            xcopy(dy, 5).start()
        xcopy(dy, 7 + k).start()

    eighth = tok // 8

    def rows(h):
        first, n, _ = CHUNKS[h]
        return pl.ds(first * eighth, n * eighth)

    def gcopy(h, k):
        up = k < 4
        hop = k % 4
        src = (NZ - hop) % NZ if up else hop
        dst = NZ - hop - 1 if up else hop + 1
        source = g_hbm if hop == 0 else gbuf.at[src]
        return rcopy(
            source.at[rows(h)], gbuf.at[dst, rows(h)], gsend.at[h, k], grecv.at[h, k], at_z(1 if up else -1)
        )

    def last(h):
        return 3 if CHUNKS[h][2] else 7

    def gather0(h):
        gcopy(h, 0).start()
        gcopy(h, 4).start()

    def gathered(h, k):
        gcopy(h, k).wait_recv()
        if k % 4 < 2 or k + 1 == last(h):
            gcopy(h, k + 1).start()

    for kind, n in FIRST:
        gather0(n) if kind else spread(n)

    for c in poles_in:
        c.wait()
    a_t = a_ref[...]
    r_t = r_ref[...]
    seg = lax.broadcasted_iota(jnp.int32, (SEG, wid), 0)
    for n in range(modes):
        a1 = jnp.broadcast_to(a_t[n : n + 1], (SEG, wid))
        ab[n] = a1
        rb[n] = jnp.broadcast_to(r_t[n : n + 1], (SEG, wid))
        p = a1
        for _ in range(5):
            p = p * p
        p2 = p * p
        p4 = p2 * p2
        m1[n] = jnp.where(seg < SEG - 1, p, 0.0)
        m2[n] = jnp.where(seg < SEG - 2, p2, 0.0)
        m4[n] = jnp.where(seg < SEG - 4, p4, 0.0)
        left = SEG - 1 - seg
        a7[n] = (
            jnp.where(left % 2 == 1, p, 1.0)
            * jnp.where((left // 2) % 2 == 1, p2, 1.0)
            * jnp.where(left // 4 == 1, p4, 1.0)
        )
    b = a_t
    for _ in range(8):
        b = b * b
    bpow[...] = b

    def partial(dy, h):
        g = jnp.concatenate([gbuf[o, rows(h)] for o in range(NZ)], axis=1)
        w = jnp.concatenate([wbuf[dy, :, o].reshape(wid, wid) for o in range(NZ)], axis=1)
        pbuf[dy, rows(h)] = lax.dot_general(
            g, w, (((1,), (1,)), ((), ())), preferred_element_type=f32
        )

    def quart(h, side):
        first, n, _ = CHUNKS[h]
        return pl.ds(first * eighth + side * (n * eighth // 2), n * eighth // 2)

    def far(h, side):
        return rcopy(
            pbuf.at[2, quart(h, side)], hbuf.at[side, quart(h, 0)],
            ysend.at[0, side, h], yrecv.at[0, side, h], at_y(1 - 2 * side),
        )

    def near(h, side, late):
        part = quart(h, side if late else 1 - side)
        return rcopy(
            pbuf.at[1 + 2 * side, part], rbuf.at[side, part],
            ysend.at[1 + late, side, h], yrecv.at[1 + late, side, h], at_y(1 - 2 * side),
        )

    def summed(dy, h):
        partial(dy, h)
        if dy == 2:
            far(h, 0).start()
            far(h, 1).start()
        elif dy:
            near(h, dy // 2, 0).start()

    def added(h, side):
        far(h, side).wait_recv()
        pbuf[1 + 2 * side, quart(h, side)] += hbuf[side, quart(h, 0)]
        near(h, side, 1).start()

    here = False
    whole = set()
    for what, a, b in EVENTS:
        if what == ARRIVED:
            arrived(a)
        elif what == SHARED:
            shared(a, b)
        elif what == GATHERED:
            gathered(a, b)
        elif what == ADDED:
            added(a, b)
        elif what == SPREAD:
            spread(a)
        else:
            if not here:
                for c in locals_:
                    c.wait()
                here = True
            if a not in whole:
                whole.add(a)
                for k in range(6, 13):
                    xwait(a, k)
            summed(a, b)
    for h in range(NH):
        for side in range(2):
            near(h, side, 0).wait_recv()
            near(h, side, 1).wait_recv()

    mix = pbuf[0] + rbuf[0] + rbuf[1]
    conv = mix * qbuf[...].astype(f32)
    for col in range(0, wid, LANES):
        gc[col // LANES] = conv[:, col : col + LANES]
    gqb[...] = (mix * vbuf[...].astype(f32)).astype(jnp.bfloat16)
    lanes = LANES

    ends = []
    for col in range(0, wid, lanes):
        cols = slice(col, col + lanes)
        poles = [ab[n, :, cols] for n in range(modes)]

        def first(k, state, poles=poles, col=col):
            state = list(state)
            for u in range(UNROLL):
                state = sweep(gc, steps - 1 - (k * UNROLL + u), state, poles, col)
            return tuple(state)

        zero = tuple(jnp.zeros((SEG, lanes), f32) for _ in range(modes))
        state = lax.fori_loop(0, steps // UNROLL, first, zero)
        for n in range(modes):
            s = state[n]
            s = s + m1[n, :, cols] * pltpu.roll(s, SEG - 1, 0)
            s = s + m2[n, :, cols] * pltpu.roll(s, SEG - 2, 0)
            s = s + m4[n, :, cols] * pltpu.roll(s, SEG - 4, 0)
            sown[pl.ds(n, 1), cols] = s[0:1]
            ends.append(jnp.where(seg[:, :lanes] < SEG - 1, pltpu.roll(s, SEG - 1, 0), 0.0))
    states = [
        rcopy(sown, sall.at[NCTX - d], ssend.at[d], srecv.at[NCTX - d], at_ctx(d))
        for d in range(1, NCTX)
    ]
    for s in states:
        s.start()
    for col in range(0, wid, lanes):
        cols = slice(col, col + lanes)
        poles = [ab[n, :, cols] for n in range(modes)]
        gains = [rb[n, :, cols] for n in range(modes)]

        def second(k, state, poles=poles, gains=gains, col=col):
            state = list(state)
            for u in range(UNROLL):
                j = steps - 1 - (k * UNROLL + u)
                state = sweep(gc, j, state, poles, col)
                yf[col // lanes, pl.ds(j, SEG, stride=steps)] = total(
                    [g * t for g, t in zip(gains, state)]
                )
            return tuple(state)

        own_ends = tuple(ends[(col // lanes) * modes + n] for n in range(modes))
        lax.fori_loop(0, steps // UNROLL, second, own_ends)

    incoming = jnp.zeros((modes, wid), f32)
    for d in range(NCTX - 1, 0, -1):
        rcopy(sown, sall.at[d], ssend.at[d], srecv.at[d], at_ctx(d)).wait_recv()
        here = jnp.where(ctx + d < NCTX, 1.0, 0.0).astype(f32)
        incoming = bpow[...] * incoming + here * sall[d]

    for t in range(len(ends)):
        n, col = t % modes, (t // modes) * lanes
        cols = slice(col, col + lanes)
        start[n, :, cols] = rb[n, :, cols] * a7[n, :, cols] * incoming[n : n + 1, cols]

    for dy in range(NY):
        ref = block(dy, ctx, *full)
        rcopy(ref, ref, asend.at[dy], arecv.at[dy], at_twin).wait_send()
        for k in range(13):
            xcopy(dy, k).wait_send()
    for k in range(8):
        for h in range(NH):
            if k % 4 < 3 or k == last(h):
                gcopy(h, k).wait_send()
    for h in range(NH):
        for side in range(2):
            far(h, side).wait_send()
            near(h, side, 0).wait_send()
            near(h, side, 1).wait_send()
    for s in states:
        s.wait_send()


def finish(gqb, yf, ab, start, gq_hbm, gi_hbm, ys, gib, sem):
    modes, _, wid = ab.shape
    tok = gqb.shape[0]
    steps = tok // SEG
    out_q = pltpu.make_async_copy(gqb, gq_hbm, sem.at[0])
    out_q.start()
    for col in range(0, wid, LANES):
        cols = slice(col, col + LANES)
        poles = [ab[n, :, cols] for n in range(modes)]

        def third(k, state, poles=poles, col=col):
            state = list(state)
            for u in range(UNROLL):
                at = pl.ds(steps - 1 - (k * UNROLL + u), SEG, stride=steps)
                state = [p * t for p, t in zip(poles, state)]
                ys[col // LANES, at] = yf[col // LANES, at] + total(state)
            return tuple(state)

        lax.fori_loop(0, steps // UNROLL, third, tuple(start[n, :, cols] for n in range(modes)))
        gib[:, cols] = ys[col // LANES].astype(gib.dtype)
    out_i = pltpu.make_async_copy(gib, gi_hbm, sem.at[1])
    out_i.start()
    out_q.wait()
    out_i.wait()


def local(out_grad, out_weight, query_in, conv_out, residues, decay_rates):
    tok, wid = query_in.shape
    modes = residues.shape[1]
    bf16, f32 = jnp.bfloat16, jnp.float32
    chunk = wid // NCTX
    w = out_weight.reshape(out_weight.shape[0] // chunk, chunk, out_weight.shape[1])
    any_ = pl.BlockSpec(memory_space=pltpu.HBM)
    vm = pl.BlockSpec(memory_space=pltpu.VMEM)
    dma = pltpu.SemaphoreType.DMA
    table = pltpu.VMEM((modes, SEG, wid), f32)
    full = jax.ShapeDtypeStruct((tok, wid), bf16)
    tall = jax.ShapeDtypeStruct((modes, SEG, wid), f32)
    inputs = (out_grad, w, query_in, conv_out, residues.T, decay_rates.T)
    held = pl.pallas_call(
        kernel,
        out_shape=(full, jax.ShapeDtypeStruct((wid // LANES, tok, LANES), f32), tall, tall),
        in_specs=[any_] * 6,
        out_specs=(vm,) * 4,
        scratch_shapes=[
            pltpu.VMEM((wid // LANES, tok, LANES), f32),
            table,
            pltpu.VMEM((NZ, tok, wid), bf16),
            pltpu.VMEM((NY, NCTX, NZ, chunk, wid), bf16),
            pltpu.VMEM((NY, tok, wid), f32),
            pltpu.VMEM((2, tok, wid), f32),
            pltpu.VMEM((2, tok, wid), f32),
            pltpu.VMEM((tok, wid), bf16),
            pltpu.VMEM((tok, wid), bf16),
            pltpu.VMEM((modes, wid), f32),
            pltpu.VMEM((modes, wid), f32),
            table, table, table, table,
            pltpu.VMEM((modes, wid), f32),
            pltpu.VMEM((modes, wid), f32),
            pltpu.VMEM((NCTX, modes, wid), f32),
            dma((9,)),
            dma((NY,)), dma((NY,)),
            dma((NH, 8)), dma((NH, 8)),
            dma((NY, 13)), dma((NY, 13)),
            dma((3, 2, NH)), dma((3, 2, NH)),
            dma((NCTX,)), dma((NCTX,)),
        ],
        compiler_params=pltpu.CompilerParams(
            collective_id=0, has_side_effects=True, vmem_limit_bytes=55_000_000
        ),
        name="mix",
    )(*[pltpu.with_memory_space_constraint(t, pltpu.HBM) for t in inputs])
    return pl.pallas_call(
        finish,
        out_shape=(full, full),
        in_specs=[vm] * 4,
        out_specs=(any_, any_),
        scratch_shapes=[
            pltpu.VMEM((wid // LANES, tok, LANES), f32),
            pltpu.VMEM((tok, wid), bf16),
            dma((2,)),
        ],
        compiler_params=pltpu.CompilerParams(vmem_limit_bytes=16 * 1024 * 1024),
        name="finish",
    )(*held)


def solution(mesh):
    placed = (
        P("ctx", "ch"),
        P(None, "ch"),
        P("ctx", "ch"),
        P("ctx", "ch"),
        P("ch", None),
        P("ch", None),
    )
    return jax.shard_map(
        local,
        mesh=mesh,
        in_specs=placed,
        out_specs=(P("ctx", "ch"), P("ctx", "ch")),
        check_vma=False,
    )
```

```python
import jax
import jax.numpy as jnp
from jax import lax
from jax.experimental import pallas as pl
from jax.experimental.pallas import tpu as pltpu
from jax.sharding import PartitionSpec as P

MESH = pl.DeviceIdType.MESH
NY, NZ, NX, NCTX = 4, 8, 4, 8
SEG = 8
LANES = 128
UNROLL = 8
NH = 2
CHUNKS = ((0, 4, True), (4, 4, False))
FIRST = ((0, 2), (0, 1), (0, 3), (1, 0), (1, 1))
ARRIVED, SHARED, GATHERED, SUMMED, ADDED, SPREAD = range(6)
EVENTS = (
    (0, 2, 0), (1, 2, 2), (0, 1, 0), (1, 2, 0), (2, 0, 0), (5, 0, 0), (2, 0, 4), (1, 2, 1), (1, 2, 3),
    (2, 1, 0), (2, 1, 4), (1, 2, 5), (0, 3, 0), (1, 1, 0), (2, 0, 1), (1, 1, 2), (1, 1, 1), (1, 1, 3),
    (1, 2, 4), (1, 3, 2), (2, 0, 5), (1, 3, 0), (1, 3, 3), (2, 1, 1), (2, 1, 5), (1, 3, 1), (1, 1, 5),
    (2, 0, 2), (2, 0, 6), (1, 1, 4), (1, 3, 5), (0, 0, 0), (2, 1, 2), (2, 1, 6), (1, 3, 4), (2, 0, 3),
    (3, 2, 0), (3, 1, 0), (3, 3, 0), (1, 0, 2), (1, 0, 0), (2, 1, 7), (3, 2, 1), (3, 1, 1), (3, 3, 1),
    (4, 0, 0), (4, 0, 1), (4, 1, 0), (4, 1, 1), (1, 0, 5), (1, 0, 4), (1, 0, 3), (1, 0, 1), (3, 0, 0),
)


def sweep(gc, j, state, poles, col):
    row = gc[col // LANES, pl.ds(j, SEG, stride=gc.shape[1] // SEG)]
    return [p * s + row for p, s in zip(poles, state)]


def total(terms):
    while len(terms) > 1:
        terms = [terms[m] + terms[m + 1] for m in range(0, len(terms), 2)]
    return terms[0]


def kernel(
    g_hbm, w_hbm, q_hbm, v_hbm, r_hbm, a_hbm,
    gqb, yf, ab, start,
    gc, rb, gbuf, wbuf, pbuf, hbuf, rbuf, qbuf, vbuf, r_ref, a_ref,
    m1, m2, m4, a7, bpow, sown, sall,
    lsem, asend, arecv, gsend, grecv, xsend, xrecv, ysend, yrecv, ssend, srecv,
):
    f32 = jnp.float32
    ctx = lax.axis_index("ctx")
    ch = lax.axis_index("ch")
    y = ch // NZ
    z = ch % NZ
    tok, wid = q_hbm.shape
    modes = a_hbm.shape[0]
    steps = tok // SEG

    def at_z(d):
        return (ctx, y * NZ + (z + d + NZ) % NZ)

    def at_y(d):
        return (ctx, ((y + d + NY) % NY) * NZ + z)

    def at_ctx(d):
        return ((ctx + d + NCTX) % NCTX, ch)

    twin = ctx + 1 - 2 * (ctx % 2)
    at_twin = (twin, ch)

    locals_ = [
        pltpu.make_async_copy(g_hbm, gbuf.at[0], lsem.at[0]),
        pltpu.make_async_copy(q_hbm, qbuf, lsem.at[1]),
        pltpu.make_async_copy(v_hbm, vbuf, lsem.at[2]),
    ]
    for dy in range(NY):
        first = (((y + dy) % NY) * NZ + z) * NCTX
        locals_.append(
            pltpu.make_async_copy(w_hbm.at[pl.ds(first, NCTX)], wbuf.at[dy, :, 0], lsem.at[3 + dy])
        )
    poles_in = [
        pltpu.make_async_copy(r_hbm, r_ref, lsem.at[7]),
        pltpu.make_async_copy(a_hbm, a_ref, lsem.at[8]),
    ]
    barrier = pltpu.get_barrier_semaphore()
    peers = [at_z(d) for d in range(1, NZ)] + [at_y(1), at_y(-1)]
    peers += [at_ctx(d) for d in range(1, NCTX)]
    for p in peers:
        pl.semaphore_signal(barrier, inc=1, device_id=p, device_id_type=MESH)
    for c in locals_ + poles_in:
        c.start()
    pl.semaphore_wait(barrier, len(peers))

    def rcopy(src, dst, ssem, rsem, dev):
        return pltpu.make_async_remote_copy(
            src_ref=src, dst_ref=dst, send_sem=ssem, recv_sem=rsem, device_id=dev, device_id_type=MESH
        )

    def spread(dy):
        for o in (4, 3, 5, 2, 6, 1, 7):
            zz = (z - o + NZ) % NZ
            row = (((y + dy) % NY) * NZ + zz) * NCTX + ctx
            rcopy(w_hbm.at[row], wbuf.at[dy, ctx, o], asend.at[dy], arecv.at[dy], at_z(-o)).start()

    def block(dy, who, lo, n):
        return wbuf.at[dy, who, pl.ds(lo, n)]

    full = (1, NZ - 1)
    part_a = (1, 4)
    part_b = (5, 3)

    def beside(who):
        return (who + NCTX - 2) % NCTX, (who + 2) % NCTX, (who + 4) % NCTX

    back, ahead, far_off = beside(ctx)
    up, down = at_ctx(2), at_ctx(-2)
    links = (
        (ctx, part_a, up), (ctx, part_b, up), (ctx, part_b, down), (ctx, part_a, down),
        (back, part_a, up), (ahead, part_b, down),
        (ctx, full, at_twin), (back, part_a, at_twin), (back, part_b, at_twin), (ahead, part_b, at_twin),
        (ahead, part_a, at_twin), (far_off, part_a, at_twin), (far_off, part_b, at_twin),
    )
    tback, tahead, tfar = beside(twin)
    lands = (
        (back, part_a), (back, part_b), (ahead, part_b), (ahead, part_a),
        (far_off, part_a), (far_off, part_b),
        (twin, full), (tback, part_a), (tback, part_b), (tahead, part_b),
        (tahead, part_a), (tfar, part_a), (tfar, part_b),
    )

    def xcopy(dy, k):
        who, part, dev = links[k]
        ref = block(dy, who, *part)
        return rcopy(ref, ref, xsend.at[dy, k], xrecv.at[dy, k], dev)

    def xwait(dy, k):
        who, part = lands[k]
        ref = block(dy, who, *part)
        rcopy(ref, ref, xsend.at[dy, k], xrecv.at[dy, k], at_twin).wait_recv()

    def arrived(dy):
        ref = block(dy, ctx, *full)
        rcopy(ref, ref, asend.at[dy], arecv.at[dy], at_twin).wait_recv()
        for k in (0, 2, 1, 3, 6):
            xcopy(dy, k).start()

    def shared(dy, k):
        xwait(dy, k)
        if k == 0:
            xcopy(dy, 4).start()
        if k == 2:
            xcopy(dy, 5).start()
        xcopy(dy, 7 + k).start()

    eighth = tok // 8

    def rows(h):
        first, n, _ = CHUNKS[h]
        return pl.ds(first * eighth, n * eighth)

    def gcopy(h, k):
        up = k < 4
        hop = k % 4
        src = (NZ - hop) % NZ if up else hop
        dst = NZ - hop - 1 if up else hop + 1
        source = g_hbm if hop == 0 else gbuf.at[src]
        return rcopy(
            source.at[rows(h)], gbuf.at[dst, rows(h)], gsend.at[h, k], grecv.at[h, k], at_z(1 if up else -1)
        )

    def last(h):
        return 3 if CHUNKS[h][2] else 7

    def gather0(h):
        gcopy(h, 0).start()
        gcopy(h, 4).start()

    def gathered(h, k):
        gcopy(h, k).wait_recv()
        if k % 4 < 2 or k + 1 == last(h):
            gcopy(h, k + 1).start()

    for kind, n in FIRST:
        gather0(n) if kind else spread(n)

    for c in poles_in:
        c.wait()
    a_t = a_ref[...]
    r_t = r_ref[...]
    seg = lax.broadcasted_iota(jnp.int32, (SEG, wid), 0)
    for n in range(modes):
        a1 = jnp.broadcast_to(a_t[n : n + 1], (SEG, wid))
        ab[n] = a1
        rb[n] = jnp.broadcast_to(r_t[n : n + 1], (SEG, wid))
        p = a1
        for _ in range(5):
            p = p * p
        p2 = p * p
        p4 = p2 * p2
        m1[n] = jnp.where(seg < SEG - 1, p, 0.0)
        m2[n] = jnp.where(seg < SEG - 2, p2, 0.0)
        m4[n] = jnp.where(seg < SEG - 4, p4, 0.0)
        left = SEG - 1 - seg
        a7[n] = (
            jnp.where(left % 2 == 1, p, 1.0)
            * jnp.where((left // 2) % 2 == 1, p2, 1.0)
            * jnp.where(left // 4 == 1, p4, 1.0)
        )
    b = a_t
    for _ in range(8):
        b = b * b
    bpow[...] = b

    def partial(dy, part):
        g = jnp.concatenate([gbuf[o, part] for o in range(NZ)], axis=1)
        w = jnp.concatenate([wbuf[dy, :, o].reshape(wid, wid) for o in range(NZ)], axis=1)
        pbuf[dy, part] = lax.dot_general(
            g, w, (((1,), (1,)), ((), ())), preferred_element_type=f32
        )

    def quart(h, side):
        first, n, _ = CHUNKS[h]
        return pl.ds(first * eighth + side * (n * eighth // 2), n * eighth // 2)

    def far(h, side):
        return rcopy(
            pbuf.at[2, quart(h, side)], hbuf.at[side, quart(h, 0)],
            ysend.at[0, side, h], yrecv.at[0, side, h], at_y(1 - 2 * side),
        )

    def near(h, side, late):
        part = quart(h, side if late else 1 - side)
        return rcopy(
            pbuf.at[1 + 2 * side, part], rbuf.at[side, part],
            ysend.at[1 + late, side, h], yrecv.at[1 + late, side, h], at_y(1 - 2 * side),
        )

    def summed(dy, h):
        partial(dy, rows(h) if dy else pl.ds(0, tok))
        if dy == 2:
            far(h, 0).start()
            far(h, 1).start()
        elif dy:
            near(h, dy // 2, 0).start()

    def added(h, side):
        far(h, side).wait_recv()
        pbuf[1 + 2 * side, quart(h, side)] += hbuf[side, quart(h, 0)]
        near(h, side, 1).start()

    here = False
    whole = set()
    for what, a, b in EVENTS:
        if what == ARRIVED:
            arrived(a)
        elif what == SHARED:
            shared(a, b)
        elif what == GATHERED:
            gathered(a, b)
        elif what == ADDED:
            added(a, b)
        elif what == SPREAD:
            spread(a)
        else:
            if not here:
                for c in locals_:
                    c.wait()
                here = True
            if a not in whole:
                whole.add(a)
                for k in range(6, 13):
                    xwait(a, k)
            summed(a, b)
    for h in range(NH):
        for side in range(2):
            near(h, side, 0).wait_recv()
            near(h, side, 1).wait_recv()

    mix = pbuf[0] + rbuf[0] + rbuf[1]
    conv = mix * qbuf[...].astype(f32)
    for col in range(0, wid, LANES):
        gc[col // LANES] = conv[:, col : col + LANES]
    gqb[...] = (mix * vbuf[...].astype(f32)).astype(jnp.bfloat16)
    lanes = LANES

    ends = []
    for col in range(0, wid, lanes):
        cols = slice(col, col + lanes)
        poles = [ab[n, :, cols] for n in range(modes)]

        def first(k, state, poles=poles, col=col):
            state = list(state)
            for u in range(UNROLL):
                state = sweep(gc, steps - 1 - (k * UNROLL + u), state, poles, col)
            return tuple(state)

        zero = tuple(jnp.zeros((SEG, lanes), f32) for _ in range(modes))
        state = lax.fori_loop(0, steps // UNROLL, first, zero)
        for n in range(modes):
            s = state[n]
            s = s + m1[n, :, cols] * pltpu.roll(s, SEG - 1, 0)
            s = s + m2[n, :, cols] * pltpu.roll(s, SEG - 2, 0)
            s = s + m4[n, :, cols] * pltpu.roll(s, SEG - 4, 0)
            sown[pl.ds(n, 1), cols] = s[0:1]
            ends.append(jnp.where(seg[:, :lanes] < SEG - 1, pltpu.roll(s, SEG - 1, 0), 0.0))
    states = [
        rcopy(sown, sall.at[NCTX - d], ssend.at[d], srecv.at[NCTX - d], at_ctx(d))
        for d in range(1, NCTX)
    ]
    for s in states:
        s.start()
    for col in range(0, wid, lanes):
        cols = slice(col, col + lanes)
        poles = [ab[n, :, cols] for n in range(modes)]
        gains = [rb[n, :, cols] for n in range(modes)]

        def second(k, state, poles=poles, gains=gains, col=col):
            state = list(state)
            for u in range(UNROLL):
                j = steps - 1 - (k * UNROLL + u)
                state = sweep(gc, j, state, poles, col)
                yf[col // lanes, pl.ds(j, SEG, stride=steps)] = total(
                    [g * t for g, t in zip(gains, state)]
                )
            return tuple(state)

        own_ends = tuple(ends[(col // lanes) * modes + n] for n in range(modes))
        lax.fori_loop(0, steps // UNROLL, second, own_ends)

    incoming = jnp.zeros((modes, wid), f32)
    for d in range(NCTX - 1, 0, -1):
        rcopy(sown, sall.at[d], ssend.at[d], srecv.at[d], at_ctx(d)).wait_recv()
        here = jnp.where(ctx + d < NCTX, 1.0, 0.0).astype(f32)
        incoming = bpow[...] * incoming + here * sall[d]

    for t in range(len(ends)):
        n, col = t % modes, (t // modes) * lanes
        cols = slice(col, col + lanes)
        start[n, :, cols] = rb[n, :, cols] * a7[n, :, cols] * incoming[n : n + 1, cols]

    for dy in range(NY):
        ref = block(dy, ctx, *full)
        rcopy(ref, ref, asend.at[dy], arecv.at[dy], at_twin).wait_send()
        for k in range(13):
            xcopy(dy, k).wait_send()
    for k in range(8):
        for h in range(NH):
            if k % 4 < 3 or k == last(h):
                gcopy(h, k).wait_send()
    for h in range(NH):
        for side in range(2):
            far(h, side).wait_send()
            near(h, side, 0).wait_send()
            near(h, side, 1).wait_send()
    for s in states:
        s.wait_send()


def finish(gqb, yf, ab, start, gq_hbm, gi_hbm, ys, gib, sem):
    modes, _, wid = ab.shape
    tok = gqb.shape[0]
    steps = tok // SEG
    out_q = pltpu.make_async_copy(gqb, gq_hbm, sem.at[0])
    out_q.start()
    for col in range(0, wid, LANES):
        cols = slice(col, col + LANES)
        poles = [ab[n, :, cols] for n in range(modes)]

        def third(k, state, poles=poles, col=col):
            state = list(state)
            for u in range(UNROLL):
                at = pl.ds(steps - 1 - (k * UNROLL + u), SEG, stride=steps)
                state = [p * t for p, t in zip(poles, state)]
                ys[col // LANES, at] = yf[col // LANES, at] + total(state)
            return tuple(state)

        lax.fori_loop(0, steps // UNROLL, third, tuple(start[n, :, cols] for n in range(modes)))
        gib[:, cols] = ys[col // LANES].astype(gib.dtype)
    out_i = pltpu.make_async_copy(gib, gi_hbm, sem.at[1])
    out_i.start()
    out_q.wait()
    out_i.wait()


def local(out_grad, out_weight, query_in, conv_out, residues, decay_rates):
    tok, wid = query_in.shape
    modes = residues.shape[1]
    bf16, f32 = jnp.bfloat16, jnp.float32
    chunk = wid // NCTX
    w = out_weight.reshape(out_weight.shape[0] // chunk, chunk, out_weight.shape[1])
    any_ = pl.BlockSpec(memory_space=pltpu.HBM)
    vm = pl.BlockSpec(memory_space=pltpu.VMEM)
    dma = pltpu.SemaphoreType.DMA
    table = pltpu.VMEM((modes, SEG, wid), f32)
    full = jax.ShapeDtypeStruct((tok, wid), bf16)
    tall = jax.ShapeDtypeStruct((modes, SEG, wid), f32)
    inputs = (out_grad, w, query_in, conv_out, residues.T, decay_rates.T)
    held = pl.pallas_call(
        kernel,
        out_shape=(full, jax.ShapeDtypeStruct((wid // LANES, tok, LANES), f32), tall, tall),
        in_specs=[any_] * 6,
        out_specs=(vm,) * 4,
        scratch_shapes=[
            pltpu.VMEM((wid // LANES, tok, LANES), f32),
            table,
            pltpu.VMEM((NZ, tok, wid), bf16),
            pltpu.VMEM((NY, NCTX, NZ, chunk, wid), bf16),
            pltpu.VMEM((NY, tok, wid), f32),
            pltpu.VMEM((2, tok, wid), f32),
            pltpu.VMEM((2, tok, wid), f32),
            pltpu.VMEM((tok, wid), bf16),
            pltpu.VMEM((tok, wid), bf16),
            pltpu.VMEM((modes, wid), f32),
            pltpu.VMEM((modes, wid), f32),
            table, table, table, table,
            pltpu.VMEM((modes, wid), f32),
            pltpu.VMEM((modes, wid), f32),
            pltpu.VMEM((NCTX, modes, wid), f32),
            dma((9,)),
            dma((NY,)), dma((NY,)),
            dma((NH, 8)), dma((NH, 8)),
            dma((NY, 13)), dma((NY, 13)),
            dma((3, 2, NH)), dma((3, 2, NH)),
            dma((NCTX,)), dma((NCTX,)),
        ],
        compiler_params=pltpu.CompilerParams(
            collective_id=0, has_side_effects=True, vmem_limit_bytes=55_000_000
        ),
        name="mix",
    )(*[pltpu.with_memory_space_constraint(t, pltpu.HBM) for t in inputs])
    return pl.pallas_call(
        finish,
        out_shape=(full, full),
        in_specs=[vm] * 4,
        out_specs=(any_, any_),
        scratch_shapes=[
            pltpu.VMEM((wid // LANES, tok, LANES), f32),
            pltpu.VMEM((tok, wid), bf16),
            dma((2,)),
        ],
        compiler_params=pltpu.CompilerParams(vmem_limit_bytes=16 * 1024 * 1024),
        name="finish",
    )(*held)


def solution(mesh):
    placed = (
        P("ctx", "ch"),
        P(None, "ch"),
        P("ctx", "ch"),
        P("ctx", "ch"),
        P("ch", None),
        P("ch", None),
    )
    return jax.shard_map(
        local,
        mesh=mesh,
        in_specs=placed,
        out_specs=(P("ctx", "ch"), P("ctx", "ch")),
        check_vma=False,
    )
```
